32 devices in a mesh: grp: 2 (over y), col: 4 (over z), row: 2 (over x), seq: 2 (over core).
Axes of the slice: x: 2, y: 2, z: 4, core: 2. Of those that a mesh axis runs over, the one named last changes fastest.
Arguments:
- alignment_tensor: float32 [192, 2, 128, 64], P(('grp', 'seq'), 'row', 'col'), parts along dimension 0, may hold values from -6 to 6
- residue_couplings: float32 [512, 256, 128], P(('grp', 'row'), 'col'), parts along dimension 0, may hold values from -6 to 6
- first_factor_matrix: float32 [64, 32], replicated, may hold values from -0.75 to 0.75
- second_factor_matrix: float32 [64, 32], replicated, may hold values from -0.75 to 0.75
- tensor_product_matrix: float32 [1024, 128], replicated, may hold values from -0.1875 to 0.1875
- coupling_score_matrix: float32 [128, 8], replicated, may hold values from -10.606602 to 10.606602
- averaged_source_matrix: float32 [64, 256], replicated, may hold values from -0.75 to 0.75
- sigmoid_matrix: float32 [64, 256], replicated, may hold values from -0.75 to 0.75
- final_matrix: float32 [256, 64], replicated, may hold values from -0.375 to 0.375
Outputs:
- revised_alignment: float32 [192, 2, 128, 64], P(('grp', 'seq'), 'row', 'col'), parts along dimension 0
- revised_couplings: float32 [512, 256, 128], P(('grp', 'row'), 'col'), parts along dimension 0
The draws below stay inside these ranges and needn't reach their ends.
There are 2 independent parts, one for each index of `grp`. The reference program is written for one: setup_inputs(seed, part) draws one part's arguments, and reference() takes and returns one part's arrays. A program takes and returns all parts, laid end to end along the dimension named above; an argument that names none is the same for every part. Nothing has to cross between parts.
All inputs are finite; a program needn't handle non-finite values.
Results may differ from the reference program's by a relative error of at most 0.0003.
Values sent between devices are 32-bit elements; how exact they have to be, the bound alone decides.
A program may use at most 64 MiB of HBM per device.

```python
import jax
import jax.numpy as jnp
from jax import lax

ALIGN_DIM = 64
CZ = 128
PRODUCT_DIM = 32
HEAD_NUMBER = 8
HEAD_DIM = 32
N = 256
ALIGNED_SEQS = 96
RESIDUE_TILES = 2
TILE_RESIDUES = 128


def draw_coupling_score_matrix(key, part):
    base = jnp.clip(jax.random.normal(jax.random.fold_in(key, 11), (CZ, HEAD_NUMBER), jnp.float32), -4.0, 4.0)
    return base * (1.5 * CZ ** (-0.5))


def draw_residue_couplings(key, part):
    noise = jnp.clip(jax.random.normal(jax.random.fold_in(key, 21), (N, N, CZ), jnp.float32), -6.0, 6.0)
    return noise


def steps_of(key, shape, cuts, least, high):
    level, own = 1.0, jax.random.fold_in(key, 6)
    for dim, blocks in cuts:
        heights = jnp.exp(jax.random.uniform(jax.random.fold_in(own, dim), (blocks,), jnp.float32, least / len(cuts), high / len(cuts)))
        level = level * jnp.repeat(heights, shape[dim] // blocks).reshape([-1 if axis == dim else 1 for axis in range(len(shape))])
    return level


def normal_values(own_key, extent, deviation, reach, pieces=(), held_as=jnp.bfloat16):
    array = deviation * jax.random.normal(own_key, extent, jnp.float32)
    if pieces:
        array = array * steps_of(own_key, extent, pieces, -0.22, 0.18)
    return jnp.clip(array, -reach, reach).astype(held_as)


def setup_inputs(seed: int = 0, part: int = 0) -> dict:
    keys = jax.random.split(jax.random.key(seed), 10)
    part_keys = jax.random.split(jax.random.fold_in(keys[9], part), 10)
    alignment_tensor = normal_values(part_keys[0], (ALIGNED_SEQS, RESIDUE_TILES, TILE_RESIDUES, ALIGN_DIM), 1.0, 6.0, ((0, 2), (1, 2), (2, 4)), jnp.float32)
    residue_couplings = draw_residue_couplings(jax.random.fold_in(jax.random.fold_in(keys[9], part), 71), part)
    first_factor_matrix = normal_values(keys[2], (ALIGN_DIM, PRODUCT_DIM), ALIGN_DIM ** -0.5, 0.75, (), jnp.float32)
    second_factor_matrix = normal_values(keys[3], (ALIGN_DIM, PRODUCT_DIM), ALIGN_DIM ** -0.5, 0.75, (), jnp.float32)
    tensor_product_matrix = normal_values(keys[4], (PRODUCT_DIM * PRODUCT_DIM, CZ), (PRODUCT_DIM * PRODUCT_DIM) ** -0.5, 0.1875, (), jnp.float32)
    coupling_score_matrix = draw_coupling_score_matrix(jax.random.fold_in(keys[9], 71), part)
    averaged_source_matrix = normal_values(keys[6], (ALIGN_DIM, HEAD_NUMBER * HEAD_DIM), ALIGN_DIM ** -0.5, 0.75, (), jnp.float32)
    sigmoid_matrix = normal_values(keys[7], (ALIGN_DIM, HEAD_NUMBER * HEAD_DIM), ALIGN_DIM ** -0.5, 0.75, (), jnp.float32)
    final_matrix = normal_values(keys[8], (HEAD_NUMBER * HEAD_DIM, ALIGN_DIM), (HEAD_NUMBER * HEAD_DIM) ** -0.5, 0.375, (), jnp.float32)
    return dict(alignment_tensor=alignment_tensor, residue_couplings=residue_couplings, first_factor_matrix=first_factor_matrix, second_factor_matrix=second_factor_matrix, tensor_product_matrix=tensor_product_matrix, coupling_score_matrix=coupling_score_matrix, averaged_source_matrix=averaged_source_matrix, sigmoid_matrix=sigmoid_matrix, final_matrix=final_matrix)


epsilon = 1e-05
exact_arithmetic = lax.Precision.HIGHEST

def standardize_entries(inputs):
    center = inputs - lax.optimization_barrier(jnp.mean(inputs, axis=-1, keepdims=True))
    spread = lax.optimization_barrier(jnp.mean(center * center, axis=-1, keepdims=True))
    return center / jnp.sqrt(spread + epsilon)

def reference(alignment_tensor, residue_couplings, first_factor_matrix, second_factor_matrix, tensor_product_matrix, coupling_score_matrix, averaged_source_matrix, sigmoid_matrix, final_matrix):
    alignment_depth_number = alignment_tensor.shape[0]
    residue_number = alignment_tensor.shape[1] * alignment_tensor.shape[2]
    alignment_depth = alignment_tensor.shape[3]
    raveled_tensor_product = alignment_tensor.reshape(alignment_depth_number, residue_number, alignment_depth)
    standardized_alignment = standardize_entries(raveled_tensor_product)
    first_factor_tile = jnp.einsum('kgd,dl->kgl', standardized_alignment, first_factor_matrix, precision=exact_arithmetic)
    second_factor_tile = jnp.einsum('kgd,dl->kgl', standardized_alignment, second_factor_matrix, precision=exact_arithmetic)
    block_rows = min(64, residue_number)
    left_blocks = first_factor_tile.reshape(alignment_depth_number, residue_number // block_rows, block_rows, -1).transpose(1, 0, 2, 3)

    def outer_block(left_block):
        product = jnp.einsum('sic,sje->ijce', left_block, second_factor_tile, precision=exact_arithmetic) / alignment_depth_number
        flat_prod = product.reshape(block_rows * residue_number, -1)
        return jnp.dot(flat_prod, tensor_product_matrix, precision=exact_arithmetic).reshape(block_rows, residue_number, -1)
    update = lax.map(outer_block, left_blocks).reshape(residue_number, residue_number, -1)
    revised_couplings = residue_couplings + update
    scores = jnp.einsum('ijc,ch->ihj', standardize_entries(revised_couplings), coupling_score_matrix, precision=exact_arithmetic)
    weights = jax.nn.softmax(scores, axis=-1)
    head_count = coupling_score_matrix.shape[1]
    averaged_sources = jnp.einsum('pko,ol->pkl', standardized_alignment, averaged_source_matrix, precision=exact_arithmetic)
    averaged_sources = averaged_sources.reshape(alignment_depth_number, residue_number, head_count, -1)
    sigmoid_factors = jax.nn.sigmoid(jnp.einsum('pko,ol->pkl', standardized_alignment, sigmoid_matrix, precision=exact_arithmetic))
    mixed_rows = jnp.einsum('ihj,sjhd->sihd', weights, averaged_sources, precision=exact_arithmetic).reshape(alignment_depth_number, residue_number, -1)
    coupling_increment = jnp.einsum('snf,fc->snc', mixed_rows * sigmoid_factors, final_matrix, precision=exact_arithmetic)
    revised_alignment = (raveled_tensor_product + coupling_increment).reshape(alignment_tensor.shape)
    return (revised_alignment, revised_couplings)
```

```python
import functools

import jax
import jax.numpy as jnp
from jax import lax
from jax.experimental import pallas as pl
from jax.experimental.pallas import tpu as pltpu
from jax.sharding import PartitionSpec as P

epsilon = 1e-05
exact_arithmetic = lax.Precision.HIGHEST


def broadcast(block, axis, holder):
    block = jnp.where(lax.axis_index(axis) == holder, block, jnp.zeros_like(block))
    return lax.psum(block, axis)


def standardize_entries(inputs):
    center = inputs - jnp.mean(inputs, axis=-1, keepdims=True)
    spread = jnp.mean(center * center, axis=-1, keepdims=True)
    return center / jnp.sqrt(spread + epsilon)


def pair_scores(pair_rows, coupling_score_matrix):
    return jnp.einsum(
        "ijc,ch->ihj",
        standardize_entries(pair_rows),
        coupling_score_matrix,
        precision=exact_arithmetic,
    )


def general_path(
    alignment_tensor,
    residue_couplings,
    first_factor_matrix,
    second_factor_matrix,
    tensor_product_matrix,
    coupling_score_matrix,
    averaged_source_matrix,
    sigmoid_matrix,
    final_matrix,
):
    shard_alignment_entries = alignment_tensor.shape[0]
    total_seqs = shard_alignment_entries * lax.axis_size("seq")
    coupling_lines = residue_couplings.shape[0]
    col_count = residue_couplings.shape[1]
    alignment_depth = alignment_tensor.shape[3]
    outer_width = first_factor_matrix.shape[1]
    head_count = coupling_score_matrix.shape[1]
    gathered_lines = lax.all_gather(alignment_tensor, "col", axis=2, tiled=True)
    alignment_tile_entries = gathered_lines.reshape(
        shard_alignment_entries, coupling_lines, alignment_depth
    )
    standardized_alignment = standardize_entries(alignment_tile_entries)
    first_factor_tile = jnp.einsum(
        "kgd,dl->kgl", standardized_alignment, first_factor_matrix, precision=exact_arithmetic
    )
    combined_matrix = jnp.concatenate([second_factor_matrix, averaged_source_matrix], axis=1)
    first_col = lax.axis_index("col") * col_count
    root_row = first_col // coupling_lines
    offset = first_col % coupling_lines
    raw_piece = lax.dynamic_slice_in_dim(alignment_tile_entries, offset, col_count, 1)
    raw_received = broadcast(raw_piece, "row", root_row)
    received = jnp.einsum(
        "pko,ol->pkl",
        standardize_entries(raw_received),
        combined_matrix,
        precision=exact_arithmetic,
    )
    second_factor_tile = received[:, :, :outer_width]
    averaged_sources = received[:, :, outer_width:].reshape(
        shard_alignment_entries, col_count, head_count, -1
    )
    block_rows = 16
    left_blocks = first_factor_tile.reshape(
        shard_alignment_entries, coupling_lines // block_rows, block_rows, outer_width
    ).transpose(1, 0, 2, 3)

    def outer_block(left_block):
        product = (
            jnp.einsum("sic,sje->ijce", left_block, second_factor_tile, precision=exact_arithmetic)
            / total_seqs
        )
        flat_prod = product.reshape(block_rows * col_count, -1)
        return jnp.dot(flat_prod, tensor_product_matrix, precision=exact_arithmetic).reshape(
            block_rows, col_count, -1
        )

    update = lax.map(outer_block, left_blocks).reshape(coupling_lines, col_count, -1)
    revised_couplings = residue_couplings + lax.psum(update, "seq")
    scores = pair_scores(revised_couplings, coupling_score_matrix)
    local_top = jnp.max(scores, axis=2)
    score_top = lax.pmax(local_top, "col")
    score_total = lax.psum(jnp.sum(jnp.exp(scores - score_top[:, :, None]), axis=2), "col")
    weights = jnp.exp(scores - score_top[:, :, None]) / score_total[:, :, None]
    mixed_rows = jnp.einsum(
        "ihj,sjhd->sihd", weights, averaged_sources, precision=exact_arithmetic
    ).reshape(shard_alignment_entries, coupling_lines, -1)
    summed = lax.psum_scatter(mixed_rows, "col", scatter_dimension=1, tiled=True)
    shard_standardized_alignment = standardize_entries(
        alignment_tensor.reshape(shard_alignment_entries, -1, alignment_depth)
    )
    sigmoid_factors = jax.nn.sigmoid(
        jnp.einsum(
            "pko,ol->pkl", shard_standardized_alignment, sigmoid_matrix, precision=exact_arithmetic
        )
    )
    coupling_increment = jnp.einsum(
        "snf,fc->snc", summed * sigmoid_factors, final_matrix, precision=exact_arithmetic
    )
    revised_alignment = alignment_tensor + coupling_increment.reshape(alignment_tensor.shape)
    return (revised_alignment, revised_couplings)


f32, bf16 = jnp.float32, jnp.bfloat16
LANES = 128


def halves(values):
    high = values.astype(bf16)
    return high, (values - high.astype(f32)).astype(bf16)


def mm(a, b):
    return jnp.dot(a, b, preferred_element_type=f32)


def mm3(a, b):
    (a_high, a_low), (b_high, b_low) = a, b
    return mm(a_high, b_high) + (mm(a_high, b_low) + mm(a_low, b_high))


def pair_kernel(
    depth, part_ref, left_ref, right_ref, product_ref, score_ref, pair_ref, out_ref, scores_ref, high_ref, low_ref
):
    width = high_ref.shape[0]
    rows = high_ref.shape[2]
    own_cols = scores_ref.shape[0]
    all_cols = pair_ref.shape[0] // rows
    outer = right_ref.shape[0] // own_cols
    r_high, r_low = halves(right_ref[...])
    r_both = jnp.concatenate([r_high, r_low], axis=1)

    def first(step, carry):
        start = pl.multiple_of(step * 2 * rows, 2 * rows)
        l_high, l_low = halves(left_ref[:, pl.ds(start, 2 * rows)])
        product = mm(r_both, jnp.concatenate([l_high, l_high], axis=0)) + mm(r_high, l_low)
        p_high, p_low = halves(product)
        for t in range(2):
            high_ref[2 * step + t] = p_high[:, t * rows : (t + 1) * rows]
            low_ref[2 * step + t] = p_low[:, t * rows : (t + 1) * rows]
        return carry

    lax.fori_loop(0, width // 2, first, 0)
    t_high, t_low = halves(product_ref[...])
    channels = t_high.shape[0]
    t_both = jnp.concatenate([t_high, t_low], axis=0)
    c_halves = halves(score_ref[...])
    first_col = part_ref[0] * own_cols

    def second(step, carry):
        def block(ref):
            pieces = [
                ref[:, pl.ds(pl.multiple_of((2 * step + t) * outer, outer), outer), :].reshape(width * outer, rows)
                for t in range(2)
            ]
            return jnp.concatenate(pieces, axis=1)

        both = mm(t_both, block(high_ref))
        update = (both[:channels] + (both[channels:] + mm(t_high, block(low_ref)))) / depth
        for t in range(2):
            col = 2 * step + t
            pair = pair_ref[pl.ds(first_col + col, rows, stride=all_cols), :].T
            revised = pair + update[:, t * rows : (t + 1) * rows]
            out_ref[pl.ds(col, rows, stride=own_cols), :] = revised.T
            center = revised - jnp.mean(revised, axis=0, keepdims=True)
            spread = jnp.mean(center * center, axis=0, keepdims=True)
            normed = center / jnp.sqrt(spread + epsilon)
            scores_ref[col] = mm3(c_halves, halves(normed))
        return carry

    lax.fori_loop(0, own_cols // 2, second, 0)


def mix_kernel(
    heads, weights_ref, normed_ref, own_ref, raw_ref, source_ref, gate_ref, final_ref, out_ref, mixed_ref
):
    groups = normed_ref.shape[1]
    tokens = normed_ref.shape[0] * normed_ref.shape[2]
    own = own_ref.shape[1]
    wide = source_ref.shape[1]
    w_high, w_low = halves(weights_ref[...])
    w_both = jnp.concatenate([w_high, w_low], axis=0)
    entries = w_high.shape[0]
    s_high, s_low = halves(source_ref[...])
    s_twice = jnp.concatenate([s_high, s_high], axis=0)
    row_head = lax.broadcasted_iota(jnp.int32, (entries, wide), 0) // own
    lane_head = lax.broadcasted_iota(jnp.int32, (entries, wide), 1) // (wide // 2 // heads) % heads
    mask = row_head == lane_head

    def step(group, carry):
        x_high, x_low = halves(normed_ref[:, group].reshape(tokens, LANES))
        values = mm(jnp.concatenate([x_high, x_low], axis=1), s_twice) + mm(x_high, s_low)
        v_high, v_low = halves(values)
        both = mm(w_both, v_high)
        full = both[:entries] + (both[entries:] + mm(w_high, v_low))
        kept = jnp.where(mask, full, 0.0)
        mixed_ref[group] = jnp.sum(kept.reshape(heads, own, wide), axis=0)
        return carry

    lax.fori_loop(0, groups, step, 0)
    g_halves = halves(gate_ref[...])
    f_halves = halves(final_ref[...])

    def finish(chunk, carry):
        at = pl.ds(chunk * (groups // 3), groups // 3)
        own_rows = own_ref[at].reshape(-1, LANES)
        gates = jax.nn.sigmoid(mm3(halves(own_rows), g_halves))
        gated = gates * mixed_ref[at].reshape(-1, wide)
        out = raw_ref[at].reshape(-1, LANES) + mm3(halves(gated), f_halves)
        out_ref[at] = out.reshape(groups // 3, own, LANES)
        return carry

    lax.fori_loop(0, 3, finish, 0)


def twice(matrix):
    zero = jnp.zeros_like(matrix)
    return jnp.concatenate(
        [jnp.concatenate([matrix, zero], axis=1), jnp.concatenate([zero, matrix], axis=1)], axis=0
    )


def pack(values):
    half = values.shape[0] // 2
    return jnp.concatenate([values[:half], values[half:]], axis=-1)


def whole_vmem(count):
    return [pl.BlockSpec(memory_space=pltpu.VMEM)] * count


def fast_path(
    alignment_tensor,
    residue_couplings,
    first_factor_matrix,
    second_factor_matrix,
    tensor_product_matrix,
    coupling_score_matrix,
    averaged_source_matrix,
    sigmoid_matrix,
    final_matrix,
):
    seqs, _, own, depth = alignment_tensor.shape
    rows, cols, channels = residue_couplings.shape
    outer = first_factor_matrix.shape[1]
    heads = coupling_score_matrix.shape[1]
    row_size, col_size, seq_size = (lax.axis_size(a) for a in ("row", "col", "seq"))
    total = seqs * seq_size
    blocks = row_size * col_size
    half_cols = cols // seq_size
    row, col, seq = (lax.axis_index(a) for a in ("row", "col", "seq"))

    raw = alignment_tensor.reshape(seqs, own, depth)
    normed = pack(standardize_entries(raw))
    gathered = lax.all_gather(normed, ("row", "col"), axis=0, tiled=False)

    def project(block, matrix):
        both = jnp.einsum("pstk,kc->pstc", block, twice(matrix), precision=lax.Precision.HIGH)
        return both.reshape(both.shape[:3] + (2, outer))

    left = project(lax.dynamic_slice_in_dim(gathered, row * col_size, col_size, 0), first_factor_matrix)
    left = left.transpose(3, 1, 4, 0, 2).reshape(seqs, outer * rows)
    right = project(lax.dynamic_slice_in_dim(gathered, col * seq_size, seq_size, 0), second_factor_matrix)
    right = right.transpose(0, 3, 1, 2, 4).reshape(seq_size, seqs, half_cols * outer)
    left_all = lax.all_gather(left, "seq", axis=0, tiled=True)
    right_all = lax.all_to_all(right, "seq", 0, 0, tiled=True).reshape(total, half_cols * outer)
    room = -total % LANES
    left_all = jnp.pad(left_all, ((0, room), (0, 0)))
    right_all = jnp.pad(right_all, ((0, room), (0, 0))).T

    revised, scores = pl.pallas_call(
        functools.partial(pair_kernel, total),
        out_shape=(
            jax.ShapeDtypeStruct((rows * half_cols, channels), f32),
            jax.ShapeDtypeStruct((half_cols, heads, rows), f32),
        ),
        in_specs=[pl.BlockSpec(memory_space=pltpu.SMEM)] + whole_vmem(5),
        out_specs=tuple(whole_vmem(2)),
        scratch_shapes=[pltpu.VMEM((outer, half_cols * outer, rows), bf16)] * 2,
        compiler_params=pltpu.CompilerParams(vmem_limit_bytes=56 << 20),
    )(
        seq.astype(jnp.int32).reshape(1),
        left_all,
        right_all,
        tensor_product_matrix.T,
        coupling_score_matrix.T,
        residue_couplings.reshape(rows * cols, channels),
    )
    revised_couplings = lax.all_gather(revised.reshape(rows, half_cols, channels), "seq", axis=1, tiled=True)

    parted = scores.reshape(half_cols, heads, col_size, own).transpose(2, 1, 3, 0)
    parted = jnp.broadcast_to(
        parted[:, None], (col_size, seq_size, heads, own, half_cols)
    ).reshape(col_size * seq_size, heads * own, half_cols)
    received = lax.all_to_all(parted, ("col", "seq"), 0, 0, tiled=True)
    received = received.transpose(1, 0, 2).reshape(heads * own, col_size * seq_size * half_cols)
    weights = jax.nn.softmax(received, axis=-1)

    groups = seqs // 2
    wide = 2 * averaged_source_matrix.shape[1]
    packed = pl.pallas_call(
        functools.partial(mix_kernel, heads),
        out_shape=jax.ShapeDtypeStruct((groups, own, LANES), f32),
        in_specs=whole_vmem(7),
        out_specs=whole_vmem(1)[0],
        scratch_shapes=[pltpu.VMEM((groups, own, wide), f32)],
        compiler_params=pltpu.CompilerParams(vmem_limit_bytes=56 << 20),
    )(
        weights,
        gathered,
        normed,
        pack(raw),
        twice(averaged_source_matrix),
        twice(sigmoid_matrix),
        twice(final_matrix),
    )
    revised_alignment = jnp.concatenate([packed[..., :depth], packed[..., depth:]], axis=0)
    return revised_alignment.reshape(alignment_tensor.shape), revised_couplings


def on_device(alignment_tensor, residue_couplings, first_factor_matrix, *rest):
    seqs, tiles, own, depth = alignment_tensor.shape
    rows, cols, channels = residue_couplings.shape
    row_size, col_size, seq_size = (lax.axis_size(a) for a in ("row", "col", "seq"))
    fits = (
        tiles == 1
        and rows == own * col_size == LANES
        and cols == own * seq_size
        and row_size * rows == col_size * cols
        and own % 16 == 0
        and seqs % 6 == 0
        and 2 * depth == channels == LANES
        and first_factor_matrix.shape[1] % 16 == 0
        and seq_size == 2
        and seqs * seq_size <= LANES
    )
    path = fast_path if fits else general_path
    return path(alignment_tensor, residue_couplings, first_factor_matrix, *rest)


def solution(mesh):
    return jax.shard_map(
        on_device,
        mesh=mesh,
        in_specs=(
            P(("grp", "seq"), "row", "col", None),
            P(("grp", "row"), "col", None),
            P(),
            P(),
            P(),
            P(),
            P(),
            P(),
            P(),
        ),
        out_specs=(P(("grp", "seq"), "row", "col", None), P(("grp", "row"), "col", None)),
        check_vma=False,
    )
```

```python
import functools

import jax
import jax.numpy as jnp
from jax import lax
from jax.experimental import pallas as pl
from jax.experimental.pallas import tpu as pltpu
from jax.sharding import PartitionSpec as P

epsilon = 1e-05
exact_arithmetic = lax.Precision.HIGHEST


def broadcast(block, axis, holder):
    block = jnp.where(lax.axis_index(axis) == holder, block, jnp.zeros_like(block))
    return lax.psum(block, axis)


def standardize_entries(inputs):
    center = inputs - jnp.mean(inputs, axis=-1, keepdims=True)
    spread = jnp.mean(center * center, axis=-1, keepdims=True)
    return center / jnp.sqrt(spread + epsilon)


def pair_scores(pair_rows, coupling_score_matrix):
    return jnp.einsum(
        "ijc,ch->ihj",
        standardize_entries(pair_rows),
        coupling_score_matrix,
        precision=exact_arithmetic,
    )


def general_path(
    alignment_tensor,
    residue_couplings,
    first_factor_matrix,
    second_factor_matrix,
    tensor_product_matrix,
    coupling_score_matrix,
    averaged_source_matrix,
    sigmoid_matrix,
    final_matrix,
):
    shard_alignment_entries = alignment_tensor.shape[0]
    total_seqs = shard_alignment_entries * lax.axis_size("seq")
    coupling_lines = residue_couplings.shape[0]
    col_count = residue_couplings.shape[1]
    alignment_depth = alignment_tensor.shape[3]
    outer_width = first_factor_matrix.shape[1]
    head_count = coupling_score_matrix.shape[1]
    gathered_lines = lax.all_gather(alignment_tensor, "col", axis=2, tiled=True)
    alignment_tile_entries = gathered_lines.reshape(
        shard_alignment_entries, coupling_lines, alignment_depth
    )
    standardized_alignment = standardize_entries(alignment_tile_entries)
    first_factor_tile = jnp.einsum(
        "kgd,dl->kgl", standardized_alignment, first_factor_matrix, precision=exact_arithmetic
    )
    combined_matrix = jnp.concatenate([second_factor_matrix, averaged_source_matrix], axis=1)
    first_col = lax.axis_index("col") * col_count
    root_row = first_col // coupling_lines
    offset = first_col % coupling_lines
    raw_piece = lax.dynamic_slice_in_dim(alignment_tile_entries, offset, col_count, 1)
    raw_received = broadcast(raw_piece, "row", root_row)
    received = jnp.einsum(
        "pko,ol->pkl",
        standardize_entries(raw_received),
        combined_matrix,
        precision=exact_arithmetic,
    )
    second_factor_tile = received[:, :, :outer_width]
    averaged_sources = received[:, :, outer_width:].reshape(
        shard_alignment_entries, col_count, head_count, -1
    )
    block_rows = 16
    left_blocks = first_factor_tile.reshape(
        shard_alignment_entries, coupling_lines // block_rows, block_rows, outer_width
    ).transpose(1, 0, 2, 3)

    def outer_block(left_block):
        product = (
            jnp.einsum("sic,sje->ijce", left_block, second_factor_tile, precision=exact_arithmetic)
            / total_seqs
        )
        flat_prod = product.reshape(block_rows * col_count, -1)
        return jnp.dot(flat_prod, tensor_product_matrix, precision=exact_arithmetic).reshape(
            block_rows, col_count, -1
        )

    update = lax.map(outer_block, left_blocks).reshape(coupling_lines, col_count, -1)
    revised_couplings = residue_couplings + lax.psum(update, "seq")
    scores = pair_scores(revised_couplings, coupling_score_matrix)
    local_top = jnp.max(scores, axis=2)
    score_top = lax.pmax(local_top, "col")
    score_total = lax.psum(jnp.sum(jnp.exp(scores - score_top[:, :, None]), axis=2), "col")
    weights = jnp.exp(scores - score_top[:, :, None]) / score_total[:, :, None]
    mixed_rows = jnp.einsum(
        "ihj,sjhd->sihd", weights, averaged_sources, precision=exact_arithmetic
    ).reshape(shard_alignment_entries, coupling_lines, -1)
    summed = lax.psum_scatter(mixed_rows, "col", scatter_dimension=1, tiled=True)
    shard_standardized_alignment = standardize_entries(
        alignment_tensor.reshape(shard_alignment_entries, -1, alignment_depth)
    )
    sigmoid_factors = jax.nn.sigmoid(
        jnp.einsum(
            "pko,ol->pkl", shard_standardized_alignment, sigmoid_matrix, precision=exact_arithmetic
        )
    )
    coupling_increment = jnp.einsum(
        "snf,fc->snc", summed * sigmoid_factors, final_matrix, precision=exact_arithmetic
    )
    revised_alignment = alignment_tensor + coupling_increment.reshape(alignment_tensor.shape)
    return (revised_alignment, revised_couplings)


f32, bf16 = jnp.float32, jnp.bfloat16
LANES = 128


def halves(values):
    high = values.astype(bf16)
    return high, (values - high.astype(f32)).astype(bf16)


def mm(a, b):
    return jnp.dot(a, b, preferred_element_type=f32)


def mm3(a, b):
    (a_high, a_low), (b_high, b_low) = a, b
    return mm(a_high, b_high) + (mm(a_high, b_low) + mm(a_low, b_high))


def nt(a, b):
    return lax.dot_general(a, b, (((1,), (1,)), ((), ())), preferred_element_type=f32)


def nt3(a, b):
    (a_high, a_low), (b_high, b_low) = a, b
    return nt(a_high, b_high) + (nt(a_high, b_low) + nt(a_low, b_high))


def block_kernel(
    row_size,
    col_size,
    seq_size,
    heads,
    raw_ref,
    pair_ref,
    first_ref,
    second_ref,
    product_ref,
    score_ref,
    source_ref,
    gate_ref,
    final_ref,
    out_ref,
    revised_ref,
    own_s,
    partner_s,
    left_s,
    right_s,
    high_s,
    low_s,
    score_s,
    sent_s,
    received_s,
    weight_s,
    gates_s,
    mixed_s,
    block_send,
    block_recv,
    partner_send,
    partner_recv,
    score_send,
    score_recv,
    pair_sem,
):
    seqs, own, depth = raw_ref.shape
    groups = seqs // 2
    rows, cols, channels = revised_ref.shape
    outer = first_ref.shape[0] // 2
    half_cols = cols // seq_size
    total = seqs * seq_size
    wide = source_ref.shape[1]
    entries = heads * own
    members = col_size * seq_size
    row, col, seq = (lax.axis_index(a) for a in ("row", "col", "seq"))
    other_row, other_seq = 1 - row, 1 - seq
    me = col * seq_size + seq
    mine = row * col_size + col

    def normalize(step, carry):
        parts = []
        for t in range(2):
            part = standardize_entries(raw_ref[step + t * groups])
            parts.append(part)
        at = pl.ds(pl.multiple_of(step * own, own), own)
        own_s[mine, at, :] = jnp.concatenate(parts, axis=-1)
        return carry

    lax.fori_loop(0, groups, normalize, 0, unroll=4)

    barrier = pltpu.get_barrier_semaphore()

    def member(offset):
        other = lax.rem(me + offset, members)
        return {"col": other // seq_size, "seq": lax.rem(other, seq_size)}

    for offset in range(1, members):
        pl.semaphore_signal(barrier, inc=1, device_id=member(offset), device_id_type=pl.DeviceIdType.MESH)
    pl.semaphore_signal(barrier, inc=1, device_id={"row": other_row}, device_id_type=pl.DeviceIdType.MESH)
    pl.semaphore_wait(barrier, members)

    started = []

    def ship(slot, target, send, condition, to=None, sems=None):
        copy = pltpu.make_async_remote_copy(
            src_ref=own_s.at[slot],
            dst_ref=(own_s if to is None else to).at[slot],
            send_sem=send,
            recv_sem=(block_recv if sems is None else sems).at[slot],
            device_id=target,
            device_id_type=pl.DeviceIdType.MESH,
        )
        started.append((copy, condition))
        run(condition, copy.start)

    def run(condition, action):
        if condition is None:
            action()
        else:
            pl.when(condition)(action)

    def both(a, b):
        return b if a is None else (a if b is None else jnp.logical_and(a, b))

    def arrived(buffer, sems, slot):
        return pltpu.make_async_remote_copy(
            src_ref=buffer.at[slot],
            dst_ref=buffer.at[slot],
            send_sem=block_send.at[0],
            recv_sem=sems.at[slot],
            device_id={"row": other_row},
            device_id_type=pl.DeviceIdType.MESH,
        ).wait_recv

    counter = [0]

    def next_send():
        counter[0] += 1
        return block_send.at[counter[0] - 1]

    def relay(slot, rightward, leftward, exists):
        if rightward:
            ship(slot, {"col": col + 1}, next_send(), both(exists, col < col_size - 1))
        if leftward:
            ship(slot, {"col": col - 1}, next_send(), both(exists, col > 0))
        ship(slot, {"row": other_row}, next_send(), exists)
        ship(slot, {"seq": other_seq}, next_send(), exists, partner_s, partner_recv)

    relay(mine, True, True, None)
    for step in range(1, col_size):
        from_left = jnp.logical_and(col >= step, True)
        run(from_left, arrived(own_s, block_recv, mine - step))
        relay(mine - step, True, False, from_left)
        from_right = jnp.logical_and(col + step < col_size, True)
        run(from_right, arrived(own_s, block_recv, mine + step))
        relay(mine + step, False, True, from_right)

    column_row = (col * seq_size) // col_size
    column_at = lax.rem(col * seq_size, col_size)
    elsewhere = column_row != row
    here = jnp.logical_not(elsewhere)
    needed = other_row * col_size + column_at
    for t in range(seq_size):
        run(elsewhere, arrived(own_s, block_recv, needed + t))
    ship(
        other_row * col_size + column_at + other_seq,
        {"seq": other_seq},
        next_send(),
        elsewhere,
        partner_s,
        partner_recv,
    )
    for block in range(col_size):
        arrived(partner_s, partner_recv, row * col_size + block)()
    run(elsewhere, arrived(partner_s, partner_recv, needed + seq))

    first = halves(first_ref[...])
    second = halves(second_ref[...])
    first_slot = row * col_size

    def project_left(group, carry):
        at = pl.ds(pl.multiple_of(group * own, own), own)
        for source, buffer in enumerate((own_s, partner_s)):
            tokens = buffer[pl.ds(first_slot, col_size), at, :].reshape(rows, LANES)
            result = nt3(first, halves(tokens))
            for half in range(2):
                place = half * seqs + source * groups + group
                left_s[pl.ds(pl.multiple_of(place * outer, outer), outer), :] = result[
                    half * outer : (half + 1) * outer
                ]
        return carry

    lax.fori_loop(0, groups, project_left, 0, unroll=4)
    column_slot = col * seq_size + seq
    room = jnp.zeros((outer, LANES - total), f32)

    def project_right(token, carry):
        tokens = jnp.concatenate(
            [buffer[column_slot, pl.ds(token, groups, stride=own), :] for buffer in (own_s, partner_s)], axis=0
        )
        result = nt3(second, halves(tokens))
        placed = jnp.concatenate([result[:outer], result[outer:], room], axis=1)
        right_s[pl.ds(pl.multiple_of(token * outer, outer), outer), :] = placed
        return carry

    lax.fori_loop(0, half_cols, project_right, 0, unroll=4)

    r_high, r_low = halves(right_s[...])
    r_both = jnp.concatenate([r_high, r_low], axis=1)
    blank = jnp.zeros((LANES - total, 2 * rows), f32)

    def outer_step(step, carry):
        pieces = [left_s[pl.ds(2 * step + t, total, stride=outer), :] for t in range(2)]
        l_high, l_low = halves(jnp.concatenate([jnp.concatenate(pieces, axis=1), blank], axis=0))
        product = mm(r_both, jnp.concatenate([l_high, l_high], axis=0)) + mm(r_high, l_low)
        p_high, p_low = halves(product)
        for t in range(2):
            high_s[2 * step + t] = p_high[:, t * rows : (t + 1) * rows]
            low_s[2 * step + t] = p_low[:, t * rows : (t + 1) * rows]
        return carry

    lax.fori_loop(0, outer // 2, outer_step, 0)
    t_high, t_low = halves(product_ref[...])
    t_both = jnp.concatenate([t_high, t_low], axis=0)
    c_halves = halves(score_ref[...])
    first_col = seq * half_cols
    flat_pair = pair_ref.reshape(rows * cols, channels)
    flat_revised = revised_ref.reshape(rows * cols, channels)

    def pair_step(step, carry):
        def block(ref):
            pieces = [
                ref[:, pl.ds(pl.multiple_of((2 * step + t) * outer, outer), outer), :].reshape(outer * outer, rows)
                for t in range(2)
            ]
            return jnp.concatenate(pieces, axis=1)

        joint = mm(t_both, block(high_s))
        update = (joint[:channels] + (joint[channels:] + mm(t_high, block(low_s)))) / total
        for t in range(2):
            column = 2 * step + t
            at = pl.ds(first_col + column, rows, stride=cols)
            revised = flat_pair[at, :].T + update[:, t * rows : (t + 1) * rows]
            flat_revised[at, :] = revised.T
            center = revised - jnp.mean(revised, axis=0, keepdims=True)
            spread = jnp.mean(center * center, axis=0, keepdims=True)
            score_s[column] = mm3(c_halves, halves(center / jnp.sqrt(spread + epsilon)))
        return carry

    lax.fori_loop(0, half_cols // 2, pair_step, 0)

    pack_count = LANES // own
    quarter = half_cols // pack_count
    scores = score_s[...].reshape(pack_count, quarter, heads, rows)
    for block in range(col_size):
        cut = [scores[t, :, :, block * own : (block + 1) * own] for t in range(pack_count)]
        sent_s[block] = jnp.concatenate(cut, axis=-1)
    received_s[me] = sent_s[col]
    own_rows = halves(own_s[mine])
    gates_s[...] = jax.nn.sigmoid(mm3(own_rows, halves(gate_ref[...]))).reshape(groups, own, wide)
    score_copies = []
    for offset in range(1, members):
        target = member(offset)
        copy = pltpu.make_async_remote_copy(
            src_ref=sent_s.at[target["col"]],
            dst_ref=received_s.at[me],
            send_sem=score_send.at[offset],
            recv_sem=score_recv.at[me],
            device_id=target,
            device_id_type=pl.DeviceIdType.MESH,
        )
        copy.start()
        score_copies.append(copy)
    half_pair = revised_ref.at[:, pl.ds(pl.multiple_of(first_col, half_cols), half_cols), :]
    pair_copy = pltpu.make_async_remote_copy(
        src_ref=half_pair,
        dst_ref=half_pair,
        send_sem=pair_sem.at[0],
        recv_sem=pair_sem.at[1],
        device_id={"seq": other_seq},
        device_id_type=pl.DeviceIdType.MESH,
    )
    pair_copy.start()
    for offset in range(1, members):
        arrived(received_s, score_recv, lax.rem(me + offset, members))()
    for t in range(seq_size):
        run(here, arrived(own_s, block_recv, other_row * col_size + column_at + t))
    last_at = lax.rem(column_at + seq_size, col_size)
    for t in range(col_size - seq_size):
        arrived(own_s, block_recv, other_row * col_size + last_at + t)()

    logits = received_s[...].reshape(members * quarter, heads, LANES)

    def over_lanes(values, op):
        result = values
        for t in range(1, pack_count):
            result = op(result, pltpu.roll(values, t * own, 1))
        return result

    top = over_lanes(jnp.max(logits, axis=0), jnp.maximum)
    powers = jnp.exp(logits - top[None])
    weights = powers / over_lanes(jnp.sum(powers, axis=0), jnp.add)[None]
    weight_s[...] = weights.reshape(members * quarter * heads, LANES)
    lines = []
    for head in range(heads):
        turned = weight_s[pl.ds(head, members * quarter, stride=heads), :].T
        lines.append(jnp.concatenate([turned[t * own : (t + 1) * own] for t in range(pack_count)], axis=1))
    w_high, w_low = halves(jnp.concatenate(lines, axis=0))
    w_both = jnp.concatenate([w_high, w_low], axis=0)
    s_high, s_low = halves(source_ref[...])
    s_twice = jnp.concatenate([s_high, s_high], axis=0)
    row_head = lax.broadcasted_iota(jnp.int32, (entries, wide), 0) // own
    lane_head = lax.broadcasted_iota(jnp.int32, (entries, wide), 1) // (wide // 2 // heads) % heads
    mask = row_head == lane_head

    def mix_step(group, carry):
        pieces = [
            own_s[:, pl.ds(pl.multiple_of(group * own + t * quarter, quarter), quarter), :].reshape(-1, LANES)
            for t in range(pack_count)
        ]
        x_high, x_low = halves(jnp.concatenate(pieces, axis=0))
        values = mm(jnp.concatenate([x_high, x_low], axis=1), s_twice) + mm(x_high, s_low)
        v_high, v_low = halves(values)
        joint = mm(w_both, v_high)
        full = joint[:entries] + (joint[entries:] + mm(w_high, v_low))
        mixed = jnp.sum(jnp.where(mask, full, 0.0).reshape(heads, own, wide), axis=0)
        mixed_s[group] = mixed * gates_s[group]
        return carry

    lax.fori_loop(0, groups, mix_step, 0)
    result = mm3(halves(mixed_s[...].reshape(groups * own, wide)), halves(final_ref[...]))
    result = result.reshape(groups, own, LANES)
    for t in range(2):
        at = pl.ds(t * groups, groups)
        out_ref[at] = raw_ref[at] + result[:, :, t * depth : (t + 1) * depth]

    for copy, condition in started:
        run(condition, copy.wait_send)
    for copy in score_copies:
        copy.wait_send()
    pair_copy.wait_send()
    other_half = revised_ref.at[:, pl.ds(pl.multiple_of(other_seq * half_cols, half_cols), half_cols), :]
    pltpu.make_async_remote_copy(
        src_ref=other_half,
        dst_ref=other_half,
        send_sem=pair_sem.at[0],
        recv_sem=pair_sem.at[1],
        device_id={"seq": other_seq},
        device_id_type=pl.DeviceIdType.MESH,
    ).wait_recv()


def twice(matrix):
    zero = jnp.zeros_like(matrix)
    return jnp.concatenate(
        [jnp.concatenate([matrix, zero], axis=1), jnp.concatenate([zero, matrix], axis=1)], axis=0
    )


def fast_path(
    alignment_tensor,
    residue_couplings,
    first_factor_matrix,
    second_factor_matrix,
    tensor_product_matrix,
    coupling_score_matrix,
    averaged_source_matrix,
    sigmoid_matrix,
    final_matrix,
):
    seqs, _, own, depth = alignment_tensor.shape
    rows, cols, channels = residue_couplings.shape
    outer = first_factor_matrix.shape[1]
    heads = coupling_score_matrix.shape[1]
    row_size, col_size, seq_size = (lax.axis_size(a) for a in ("row", "col", "seq"))
    total = seqs * seq_size
    blocks = row_size * col_size
    half_cols = cols // seq_size
    members = col_size * seq_size
    groups = seqs // 2
    wide = 2 * averaged_source_matrix.shape[1]
    quarter = half_cols * own // LANES
    vmem = pl.BlockSpec(memory_space=pltpu.VMEM)
    dma = pltpu.SemaphoreType.DMA
    revised_alignment, revised_couplings = pl.pallas_call(
        functools.partial(block_kernel, row_size, col_size, seq_size, heads),
        out_shape=(
            jax.ShapeDtypeStruct((seqs, own, depth), f32),
            jax.ShapeDtypeStruct((rows, cols, channels), f32),
        ),
        in_specs=[vmem] * 9,
        out_specs=(vmem, vmem),
        scratch_shapes=[
            pltpu.VMEM((blocks, groups * own, LANES), f32),
            pltpu.VMEM((blocks, groups * own, LANES), f32),
            pltpu.VMEM((total * outer, rows), f32),
            pltpu.VMEM((half_cols * outer, LANES), f32),
            pltpu.VMEM((outer, half_cols * outer, rows), bf16),
            pltpu.VMEM((outer, half_cols * outer, rows), bf16),
            pltpu.VMEM((half_cols, heads, rows), f32),
            pltpu.VMEM((col_size, quarter, heads, LANES), f32),
            pltpu.VMEM((members, quarter, heads, LANES), f32),
            pltpu.VMEM((members * quarter * heads, LANES), f32),
            pltpu.VMEM((groups, own, wide), f32),
            pltpu.VMEM((groups, own, wide), f32),
            dma((32,)),
            dma((blocks,)),
            dma((1,)),
            dma((blocks,)),
            dma((members,)),
            dma((members,)),
            dma((2,)),
        ],
        compiler_params=pltpu.CompilerParams(
            collective_id=0, has_side_effects=True, vmem_limit_bytes=60 << 20
        ),
    )(
        alignment_tensor.reshape(seqs, own, depth),
        residue_couplings,
        twice(first_factor_matrix).T,
        twice(second_factor_matrix).T,
        tensor_product_matrix.T,
        coupling_score_matrix.T,
        twice(averaged_source_matrix),
        twice(sigmoid_matrix),
        twice(final_matrix),
    )
    return revised_alignment.reshape(alignment_tensor.shape), revised_couplings


def on_device(alignment_tensor, residue_couplings, first_factor_matrix, *rest):
    seqs, tiles, own, depth = alignment_tensor.shape
    rows, cols, channels = residue_couplings.shape
    row_size, col_size, seq_size = (lax.axis_size(a) for a in ("row", "col", "seq"))
    fits = (
        tiles == 1
        and rows == own * col_size == LANES
        and cols == own * seq_size
        and row_size * rows == col_size * cols
        and own % 16 == 0
        and seqs % 6 == 0
        and 2 * depth == channels == LANES
        and first_factor_matrix.shape[1] % 16 == 0
        and seq_size == row_size == 2
        and rest[2].shape[1] == 8 == own * own // LANES
        and seqs * seq_size <= LANES
    )
    path = fast_path if fits else general_path
    return path(alignment_tensor, residue_couplings, first_factor_matrix, *rest)


def solution(mesh):
    return jax.shard_map(
        on_device,
        mesh=mesh,
        in_specs=(
            P(("grp", "seq"), "row", "col", None),
            P(("grp", "row"), "col", None),
            P(),
            P(),
            P(),
            P(),
            P(),
            P(),
            P(),
        ),
        out_specs=(P(("grp", "seq"), "row", "col", None), P(("grp", "row"), "col", None)),
        check_vma=False,
    )
```

```python
import functools

import jax
import jax.numpy as jnp
from jax import lax
from jax.experimental import pallas as pl
from jax.experimental.pallas import tpu as pltpu
from jax.sharding import PartitionSpec as P

epsilon = 1e-05
exact_arithmetic = lax.Precision.HIGHEST


def broadcast(block, axis, holder):
    block = jnp.where(lax.axis_index(axis) == holder, block, jnp.zeros_like(block))
    return lax.psum(block, axis)


def standardize_entries(inputs):
    center = inputs - jnp.mean(inputs, axis=-1, keepdims=True)
    spread = jnp.mean(center * center, axis=-1, keepdims=True)
    return center / jnp.sqrt(spread + epsilon)


def pair_scores(pair_rows, coupling_score_matrix):
    return jnp.einsum(
        "ijc,ch->ihj",
        standardize_entries(pair_rows),
        coupling_score_matrix,
        precision=exact_arithmetic,
    )


def general_path(
    alignment_tensor,
    residue_couplings,
    first_factor_matrix,
    second_factor_matrix,
    tensor_product_matrix,
    coupling_score_matrix,
    averaged_source_matrix,
    sigmoid_matrix,
    final_matrix,
):
    shard_alignment_entries = alignment_tensor.shape[0]
    total_seqs = shard_alignment_entries * lax.axis_size("seq")
    coupling_lines = residue_couplings.shape[0]
    col_count = residue_couplings.shape[1]
    alignment_depth = alignment_tensor.shape[3]
    outer_width = first_factor_matrix.shape[1]
    head_count = coupling_score_matrix.shape[1]
    gathered_lines = lax.all_gather(alignment_tensor, "col", axis=2, tiled=True)
    alignment_tile_entries = gathered_lines.reshape(
        shard_alignment_entries, coupling_lines, alignment_depth
    )
    standardized_alignment = standardize_entries(alignment_tile_entries)
    first_factor_tile = jnp.einsum(
        "kgd,dl->kgl", standardized_alignment, first_factor_matrix, precision=exact_arithmetic
    )
    combined_matrix = jnp.concatenate([second_factor_matrix, averaged_source_matrix], axis=1)
    first_col = lax.axis_index("col") * col_count
    root_row = first_col // coupling_lines
    offset = first_col % coupling_lines
    raw_piece = lax.dynamic_slice_in_dim(alignment_tile_entries, offset, col_count, 1)
    raw_received = broadcast(raw_piece, "row", root_row)
    received = jnp.einsum(
        "pko,ol->pkl",
        standardize_entries(raw_received),
        combined_matrix,
        precision=exact_arithmetic,
    )
    second_factor_tile = received[:, :, :outer_width]
    averaged_sources = received[:, :, outer_width:].reshape(
        shard_alignment_entries, col_count, head_count, -1
    )
    block_rows = 16
    left_blocks = first_factor_tile.reshape(
        shard_alignment_entries, coupling_lines // block_rows, block_rows, outer_width
    ).transpose(1, 0, 2, 3)

    def outer_block(left_block):
        product = (
            jnp.einsum("sic,sje->ijce", left_block, second_factor_tile, precision=exact_arithmetic)
            / total_seqs
        )
        flat_prod = product.reshape(block_rows * col_count, -1)
        return jnp.dot(flat_prod, tensor_product_matrix, precision=exact_arithmetic).reshape(
            block_rows, col_count, -1
        )

    update = lax.map(outer_block, left_blocks).reshape(coupling_lines, col_count, -1)
    revised_couplings = residue_couplings + lax.psum(update, "seq")
    scores = pair_scores(revised_couplings, coupling_score_matrix)
    local_top = jnp.max(scores, axis=2)
    score_top = lax.pmax(local_top, "col")
    score_total = lax.psum(jnp.sum(jnp.exp(scores - score_top[:, :, None]), axis=2), "col")
    weights = jnp.exp(scores - score_top[:, :, None]) / score_total[:, :, None]
    mixed_rows = jnp.einsum(
        "ihj,sjhd->sihd", weights, averaged_sources, precision=exact_arithmetic
    ).reshape(shard_alignment_entries, coupling_lines, -1)
    summed = lax.psum_scatter(mixed_rows, "col", scatter_dimension=1, tiled=True)
    shard_standardized_alignment = standardize_entries(
        alignment_tensor.reshape(shard_alignment_entries, -1, alignment_depth)
    )
    sigmoid_factors = jax.nn.sigmoid(
        jnp.einsum(
            "pko,ol->pkl", shard_standardized_alignment, sigmoid_matrix, precision=exact_arithmetic
        )
    )
    coupling_increment = jnp.einsum(
        "snf,fc->snc", summed * sigmoid_factors, final_matrix, precision=exact_arithmetic
    )
    revised_alignment = alignment_tensor + coupling_increment.reshape(alignment_tensor.shape)
    return (revised_alignment, revised_couplings)


f32, bf16 = jnp.float32, jnp.bfloat16
LANES = 128


def halves(values):
    high = values.astype(bf16)
    return high, (values - high.astype(f32)).astype(bf16)


def mm(a, b):
    return jnp.dot(a, b, preferred_element_type=f32)


def mm3(a, b):
    (a_high, a_low), (b_high, b_low) = a, b
    return mm(a_high, b_high) + (mm(a_high, b_low) + mm(a_low, b_high))


def nt(a, b):
    return lax.dot_general(a, b, (((1,), (1,)), ((), ())), preferred_element_type=f32)


def nt3(a, b):
    (a_high, a_low), (b_high, b_low) = a, b
    return nt(a_high, b_high) + (nt(a_high, b_low) + nt(a_low, b_high))


def block_kernel(
    row_size,
    col_size,
    seq_size,
    heads,
    raw_ref,
    pair_ref,
    first_ref,
    second_ref,
    product_ref,
    score_ref,
    source_ref,
    gate_ref,
    final_ref,
    out_ref,
    revised_ref,
    own_s,
    l_s,
    r_own,
    r_s,
    left_s,
    right_s,
    high_s,
    low_s,
    score_s,
    sent_s,
    received_s,
    weight_s,
    gates_s,
    mixed_s,
    block_send,
    block_recv,
    l_recv,
    r_recv,
    local_sem,
    score_send,
    score_recv,
    pair_sem,
):
    seqs, own, depth = raw_ref.shape
    groups = seqs // 2
    rows, cols, channels = revised_ref.shape
    outer = first_ref.shape[0] // 2
    half_cols = cols // seq_size
    total = seqs * seq_size
    wide = source_ref.shape[1]
    entries = heads * own
    members = col_size * seq_size
    row, col, seq = (lax.axis_index(a) for a in ("row", "col", "seq"))
    other_row, other_seq = 1 - row, 1 - seq
    me = col * seq_size + seq
    mine = row * col_size + col

    def normalize(step, carry):
        parts = []
        for t in range(2):
            part = standardize_entries(raw_ref[step + t * groups])
            parts.append(part)
        at = pl.ds(pl.multiple_of(step * own, own), own)
        own_s[mine, at, :] = jnp.concatenate(parts, axis=-1)
        return carry

    lax.fori_loop(0, groups, normalize, 0, unroll=4)

    first = halves(first_ref[...])
    second = halves(second_ref[...])
    pairs = LANES // 2 // own
    left_steps = groups // pairs

    def project_left(step, carry):
        parts = []
        for t in range(pairs):
            at = pl.ds(pl.multiple_of((t * left_steps + step) * own, own), own)
            result = nt3(first, halves(own_s[mine, at, :]))
            parts += [result[:outer], result[outer:]]
        l_s[col, seq, pl.ds(pl.multiple_of(step * outer, outer), outer), :] = jnp.concatenate(parts, axis=1)
        return carry

    lax.fori_loop(0, left_steps, project_left, 0, unroll=4)
    span = LANES // 2
    room = jnp.zeros((outer, span - seqs), f32)
    right_steps = half_cols // 2

    def project_right(step, carry):
        parts = []
        for t in range(2):
            tokens = own_s[mine, pl.ds(t * right_steps + step, groups, stride=own), :]
            result = nt3(second, halves(tokens))
            parts += [result[:outer], result[outer:], room]
        r_own[pl.ds(pl.multiple_of(step * outer, outer), outer), :] = jnp.concatenate(parts, axis=1)
        return carry

    lax.fori_loop(0, right_steps, project_right, 0, unroll=4)

    barrier = pltpu.get_barrier_semaphore()

    def member(offset):
        other = lax.rem(me + offset, members)
        return {"col": other // seq_size, "seq": lax.rem(other, seq_size)}

    for offset in range(1, members):
        pl.semaphore_signal(barrier, inc=1, device_id=member(offset), device_id_type=pl.DeviceIdType.MESH)
    pl.semaphore_signal(barrier, inc=1, device_id={"row": other_row}, device_id_type=pl.DeviceIdType.MESH)
    pl.semaphore_wait(barrier, members)

    started = []

    def ship(source, place, target, sem, condition):
        copy = pltpu.make_async_remote_copy(
            src_ref=source,
            dst_ref=place,
            send_sem=next_send(),
            recv_sem=sem,
            device_id=target,
            device_id_type=pl.DeviceIdType.MESH,
        )
        started.append((copy, condition))
        run(condition, copy.start)

    def run(condition, action):
        if condition is None:
            action()
        else:
            pl.when(condition)(action)

    def both(a, b):
        return b if a is None else (a if b is None else jnp.logical_and(a, b))

    def arrived(place, sem):
        return pltpu.make_async_remote_copy(
            src_ref=place,
            dst_ref=place,
            send_sem=block_send.at[0],
            recv_sem=sem,
            device_id={"row": other_row},
            device_id_type=pl.DeviceIdType.MESH,
        ).wait_recv

    counter = [0]

    def next_send():
        counter[0] += 1
        return block_send.at[counter[0] - 1]

    def relay_left(at, rightward, leftward, exists):
        place, sem = l_s.at[at, seq], l_recv.at[at, seq]
        if rightward:
            ship(place, place, {"col": col + 1}, sem, both(exists, col < col_size - 1))
        if leftward:
            ship(place, place, {"col": col - 1}, sem, both(exists, col > 0))
        ship(place, place, {"seq": other_seq}, sem, exists)

    def relay(slot, rightward, leftward, across, exists):
        place, sem = own_s.at[slot], block_recv.at[slot]
        if rightward:
            ship(place, place, {"col": col + 1}, sem, both(exists, col < col_size - 1))
        if leftward:
            ship(place, place, {"col": col - 1}, sem, both(exists, col > 0))
        if across:
            ship(place, place, {"row": other_row}, sem, exists)

    def relay_step(step):
        run(col >= step, arrived(own_s.at[mine - step], block_recv.at[mine - step]))
        relay(mine - step, True, False, True, col >= step)
        run(col + step < col_size, arrived(own_s.at[mine + step], block_recv.at[mine + step]))
        relay(mine + step, False, True, True, col + step < col_size)

    relay_left(col, True, True, None)
    column_slot = col * seq_size + seq
    here = column_slot // col_size == row
    elsewhere = jnp.logical_not(here)
    target_col, target_seq = mine // seq_size, lax.rem(mine, seq_size)
    own_right = jnp.logical_and(target_col == col, target_seq == seq)
    ship(
        r_own, r_s.at[seq], {"col": target_col, "seq": target_seq}, r_recv.at[seq], jnp.logical_not(own_right)
    )
    ship(own_s.at[mine], own_s.at[mine], {"row": other_row}, block_recv.at[mine], elsewhere)

    @pl.when(own_right)
    def _():
        keep = pltpu.make_async_copy(r_own, r_s.at[seq], local_sem.at[0])
        keep.start()
        keep.wait()

    for step in range(1, col_size):
        run(col >= step, arrived(l_s.at[col - step, seq], l_recv.at[col - step, seq]))
        relay_left(col - step, True, False, col >= step)
        run(col + step < col_size, arrived(l_s.at[col + step, seq], l_recv.at[col + step, seq]))
        relay_left(col + step, False, True, col + step < col_size)
        if step == 1:
            source_here = lax.rem(column_slot, col_size) == col
            for source in range(seq_size):
                kept = jnp.logical_and(source_here, seq == source)
                run(jnp.logical_and(here, jnp.logical_not(kept)), arrived(r_s.at[source], r_recv.at[source]))
                ship(r_s.at[source], r_s.at[source], {"row": other_row}, r_recv.at[source], here)
            ship(own_s.at[mine], own_s.at[mine], {"row": other_row}, block_recv.at[mine], here)
    relay(mine, True, True, False, None)
    for source in range(seq_size):
        run(elsewhere, arrived(r_s.at[source], r_recv.at[source]))
    for at in range(col_size):
        arrived(l_s.at[at, other_seq], l_recv.at[at, other_seq])()

    blank = jnp.zeros(((span - seqs) * outer, rows), f32)
    for source in range(seq_size):
        left_s[(source * span + seqs) * outer : (source + 1) * span * outer, :] = blank

    def place_left(step, carry):
        at = pl.ds(pl.multiple_of(step * outer, outer), outer)
        for source in range(seq_size):
            blocks = [l_s[t, source, at, :] for t in range(col_size)]
            for t in range(pairs):
                for half in range(2):
                    lane = (2 * t + half) * own
                    line = jnp.concatenate([block[:, lane : lane + own] for block in blocks], axis=1)
                    place = source * span + half * groups + t * left_steps + step
                    left_s[pl.ds(pl.multiple_of(place * outer, outer), outer), :] = line
        return carry

    lax.fori_loop(0, left_steps, place_left, 0, unroll=2)
    for t in range(2):
        right_s[t * right_steps * outer : (t + 1) * right_steps * outer, :] = jnp.concatenate(
            [r_s[source, :, t * span : (t + 1) * span] for source in range(seq_size)], axis=1
        )

    r_high, r_low = halves(right_s[...])
    r_both = jnp.concatenate([r_high, r_low], axis=1)

    def outer_step(step, carry):
        pieces = [left_s[pl.ds(2 * step + t, LANES, stride=outer), :] for t in range(2)]
        l_high, l_low = halves(jnp.concatenate(pieces, axis=1))
        product = mm(r_both, jnp.concatenate([l_high, l_high], axis=0)) + mm(r_high, l_low)
        p_high, p_low = halves(product)
        for t in range(2):
            high_s[2 * step + t] = p_high[:, t * rows : (t + 1) * rows]
            low_s[2 * step + t] = p_low[:, t * rows : (t + 1) * rows]
        return carry

    lax.fori_loop(0, outer // 2, outer_step, 0)
    relay_step(1)
    t_high, t_low = halves(product_ref[...])
    t_both = jnp.concatenate([t_high, t_low], axis=0)
    c_halves = halves(score_ref[...])
    first_col = seq * half_cols
    flat_pair = pair_ref.reshape(rows * cols, channels)
    flat_revised = revised_ref.reshape(rows * cols, channels)

    def pair_step(step, carry):
        def block(ref):
            pieces = [
                ref[:, pl.ds(pl.multiple_of((2 * step + t) * outer, outer), outer), :].reshape(outer * outer, rows)
                for t in range(2)
            ]
            return jnp.concatenate(pieces, axis=1)

        joint = mm(t_both, block(high_s))
        update = (joint[:channels] + (joint[channels:] + mm(t_high, block(low_s)))) / total
        for t in range(2):
            column = 2 * step + t
            at = pl.ds(first_col + column, rows, stride=cols)
            revised = flat_pair[at, :].T + update[:, t * rows : (t + 1) * rows]
            flat_revised[at, :] = revised.T
            center = revised - jnp.mean(revised, axis=0, keepdims=True)
            spread = jnp.mean(center * center, axis=0, keepdims=True)
            score_s[column] = mm3(c_halves, halves(center / jnp.sqrt(spread + epsilon)))
        return carry

    bounds = [half_cols // 2 * t // (col_size - 1) for t in range(1, col_size)]
    lax.fori_loop(0, bounds[-2], pair_step, 0)
    for step in range(2, col_size - 1):
        relay_step(step)
    lax.fori_loop(bounds[-2], bounds[-1], pair_step, 0)

    pack_count = LANES // own
    quarter = half_cols // pack_count
    scores = score_s[...].reshape(pack_count, quarter, heads, rows)
    for block in range(col_size):
        cut = [scores[t, :, :, block * own : (block + 1) * own] for t in range(pack_count)]
        sent_s[block] = jnp.concatenate(cut, axis=-1)
    received_s[me] = sent_s[col]
    own_rows = halves(own_s[mine])
    gates_s[...] = jax.nn.sigmoid(mm3(own_rows, halves(gate_ref[...]))).reshape(groups, own, wide)
    score_copies = []
    for offset in range(1, members):
        target = member(offset)
        copy = pltpu.make_async_remote_copy(
            src_ref=sent_s.at[target["col"]],
            dst_ref=received_s.at[me],
            send_sem=score_send.at[offset],
            recv_sem=score_recv.at[me],
            device_id=target,
            device_id_type=pl.DeviceIdType.MESH,
        )
        copy.start()
        score_copies.append(copy)
    if col_size > 2:
        relay_step(col_size - 1)
    half_pair = revised_ref.at[:, pl.ds(pl.multiple_of(first_col, half_cols), half_cols), :]
    pair_copy = pltpu.make_async_remote_copy(
        src_ref=half_pair,
        dst_ref=half_pair,
        send_sem=pair_sem.at[0],
        recv_sem=pair_sem.at[1],
        device_id={"seq": other_seq},
        device_id_type=pl.DeviceIdType.MESH,
    )
    pair_copy.start()
    for offset in range(1, members):
        other = lax.rem(me + offset, members)
        arrived(received_s.at[other], score_recv.at[other])()
    logits = received_s[...].reshape(members * quarter, heads, LANES)

    def over_lanes(values, op):
        result = values
        for t in range(1, pack_count):
            result = op(result, pltpu.roll(values, t * own, 1))
        return result

    top = over_lanes(jnp.max(logits, axis=0), jnp.maximum)
    powers = jnp.exp(logits - top[None])
    weights = powers / over_lanes(jnp.sum(powers, axis=0), jnp.add)[None]
    weight_s[...] = weights.reshape(members * quarter * heads, LANES)
    lines = []
    for head in range(heads):
        turned = weight_s[pl.ds(head, members * quarter, stride=heads), :].T
        lines.append(jnp.concatenate([turned[t * own : (t + 1) * own] for t in range(pack_count)], axis=1))
    w_high, w_low = halves(jnp.concatenate(lines, axis=0))
    w_both = jnp.concatenate([w_high, w_low], axis=0)
    s_high, s_low = halves(source_ref[...])
    s_twice = jnp.concatenate([s_high, s_high], axis=0)
    row_head = lax.broadcasted_iota(jnp.int32, (entries, wide), 0) // own
    lane_head = lax.broadcasted_iota(jnp.int32, (entries, wide), 1) // (wide // 2 // heads) % heads
    mask = row_head == lane_head

    for at in range(col_size):
        arrived(own_s.at[other_row * col_size + at], block_recv.at[other_row * col_size + at])()

    def mix_step(group, carry):
        pieces = [
            own_s[:, pl.ds(pl.multiple_of(group * own + t * quarter, quarter), quarter), :].reshape(-1, LANES)
            for t in range(pack_count)
        ]
        x_high, x_low = halves(jnp.concatenate(pieces, axis=0))
        values = mm(jnp.concatenate([x_high, x_low], axis=1), s_twice) + mm(x_high, s_low)
        v_high, v_low = halves(values)
        joint = mm(w_both, v_high)
        full = joint[:entries] + (joint[entries:] + mm(w_high, v_low))
        mixed = jnp.sum(jnp.where(mask, full, 0.0).reshape(heads, own, wide), axis=0)
        mixed_s[group] = mixed * gates_s[group]
        return carry

    lax.fori_loop(0, groups, mix_step, 0)
    result = mm3(halves(mixed_s[...].reshape(groups * own, wide)), halves(final_ref[...]))
    result = result.reshape(groups, own, LANES)
    for t in range(2):
        at = pl.ds(t * groups, groups)
        out_ref[at] = raw_ref[at] + result[:, :, t * depth : (t + 1) * depth]

    for copy, condition in started:
        run(condition, copy.wait_send)
    for copy in score_copies:
        copy.wait_send()
    pair_copy.wait_send()
    other_half = revised_ref.at[:, pl.ds(pl.multiple_of(other_seq * half_cols, half_cols), half_cols), :]
    pltpu.make_async_remote_copy(
        src_ref=other_half,
        dst_ref=other_half,
        send_sem=pair_sem.at[0],
        recv_sem=pair_sem.at[1],
        device_id={"seq": other_seq},
        device_id_type=pl.DeviceIdType.MESH,
    ).wait_recv()


def twice(matrix):
    zero = jnp.zeros_like(matrix)
    return jnp.concatenate(
        [jnp.concatenate([matrix, zero], axis=1), jnp.concatenate([zero, matrix], axis=1)], axis=0
    )


def fast_path(
    alignment_tensor,
    residue_couplings,
    first_factor_matrix,
    second_factor_matrix,
    tensor_product_matrix,
    coupling_score_matrix,
    averaged_source_matrix,
    sigmoid_matrix,
    final_matrix,
):
    seqs, _, own, depth = alignment_tensor.shape
    rows, cols, channels = residue_couplings.shape
    outer = first_factor_matrix.shape[1]
    heads = coupling_score_matrix.shape[1]
    row_size, col_size, seq_size = (lax.axis_size(a) for a in ("row", "col", "seq"))
    total = seqs * seq_size
    blocks = row_size * col_size
    half_cols = cols // seq_size
    members = col_size * seq_size
    groups = seqs // 2
    wide = 2 * averaged_source_matrix.shape[1]
    quarter = half_cols * own // LANES
    vmem = pl.BlockSpec(memory_space=pltpu.VMEM)
    dma = pltpu.SemaphoreType.DMA
    revised_alignment, revised_couplings = pl.pallas_call(
        functools.partial(block_kernel, row_size, col_size, seq_size, heads),
        out_shape=(
            jax.ShapeDtypeStruct((seqs, own, depth), f32),
            jax.ShapeDtypeStruct((rows, cols, channels), f32),
        ),
        in_specs=[vmem] * 9,
        out_specs=(vmem, vmem),
        scratch_shapes=[
            pltpu.VMEM((blocks, groups * own, LANES), f32),
            pltpu.VMEM((col_size, seq_size, groups // (LANES // 2 // own) * outer, LANES), f32),
            pltpu.VMEM((half_cols // 2 * outer, LANES), f32),
            pltpu.VMEM((seq_size, half_cols // 2 * outer, LANES), f32),
            pltpu.VMEM((LANES * outer, rows), f32),
            pltpu.VMEM((half_cols * outer, LANES), f32),
            pltpu.VMEM((outer, half_cols * outer, rows), bf16),
            pltpu.VMEM((outer, half_cols * outer, rows), bf16),
            pltpu.VMEM((half_cols, heads, rows), f32),
            pltpu.VMEM((col_size, quarter, heads, LANES), f32),
            pltpu.VMEM((members, quarter, heads, LANES), f32),
            pltpu.VMEM((members * quarter * heads, LANES), f32),
            pltpu.VMEM((groups, own, wide), f32),
            pltpu.VMEM((groups, own, wide), f32),
            dma((64,)),
            dma((blocks,)),
            dma((col_size, seq_size)),
            dma((seq_size,)),
            dma((1,)),
            dma((members,)),
            dma((members,)),
            dma((2,)),
        ],
        compiler_params=pltpu.CompilerParams(
            collective_id=0, has_side_effects=True, vmem_limit_bytes=60 << 20
        ),
    )(
        alignment_tensor.reshape(seqs, own, depth),
        residue_couplings,
        twice(first_factor_matrix).T,
        twice(second_factor_matrix).T,
        tensor_product_matrix.T,
        coupling_score_matrix.T,
        twice(averaged_source_matrix),
        twice(sigmoid_matrix),
        twice(final_matrix),
    )
    return revised_alignment.reshape(alignment_tensor.shape), revised_couplings


def on_device(alignment_tensor, residue_couplings, first_factor_matrix, *rest):
    seqs, tiles, own, depth = alignment_tensor.shape
    rows, cols, channels = residue_couplings.shape
    row_size, col_size, seq_size = (lax.axis_size(a) for a in ("row", "col", "seq"))
    fits = (
        tiles == 1
        and rows == own * col_size == LANES
        and cols == own * seq_size
        and row_size * rows == col_size * cols
        and own % 16 == 0
        and seqs % 6 == 0
        and 2 * depth == channels == LANES
        and first_factor_matrix.shape[1] % 16 == 0
        and seq_size == row_size == 2
        and rest[2].shape[1] == 8 == own * own // LANES
        and seqs * seq_size <= LANES
        and seqs // 2 % (LANES // 2 // own) == 0
        and col_size > 2
    )
    path = fast_path if fits else general_path
    return path(alignment_tensor, residue_couplings, first_factor_matrix, *rest)


def solution(mesh):
    return jax.shard_map(
        on_device,
        mesh=mesh,
        in_specs=(
            P(("grp", "seq"), "row", "col", None),
            P(("grp", "row"), "col", None),
            P(),
            P(),
            P(),
            P(),
            P(),
            P(),
            P(),
        ),
        out_specs=(P(("grp", "seq"), "row", "col", None), P(("grp", "row"), "col", None)),
        check_vma=False,
    )
```
